256 devices in a mesh: ev: 256 (over y, z, x, core).
Axes of the slice: x: 4, y: 4, z: 8, core: 2. Of those that a mesh axis runs over, the one named last changes fastest.
Arguments:
- records: bfloat16 [32768, 512], P('ev'), may hold values from -16 to 16
- filter_taps: bfloat16 [65], replicated, may hold values from -0.75 to 0.75
- live_counts: int32 [256], P('ev'), may hold values from 64 to 128, as said below
- pair_valid: int32 [256, 9], P('ev'), may hold values 0 or 1
Outputs:
- correlations: bfloat16 [32768, 10, 25, 128], P('ev')
The draws below stay inside these ranges and needn't reach their ends.
Inputs may be any that keep to these rules, and one draw needn't show every extreme that they name: The first live_counts[b] events of block b are live and its other rows are padding; some block has all 128 events live.
All inputs are finite; a program needn't handle non-finite values. No bound on the sum of `pair_valid` on one device may be relied on, other than what follows from the above.
Results may differ from the reference program's by a relative error of at most 0.0047.
Values may be sent and summed in bfloat16 or wider, within the bound.
No kernel may reach another device: no remote copies, remote signals or barrier semaphores. Data moves between devices by JAX's collectives and lax.ppermute only.
A program may use at most 64 MiB of HBM per device.

```python
import math
import jax
import jax.numpy as jnp
from jax import lax

EB = 128
W = 512
TAPS = 65
HALF = 12
REACH = 9
BLOCKS = 256
EVENTS = 32768


def draw_records(key, part):
    scale_key = jax.random.fold_in(key, 11)
    shape_key = jax.random.fold_in(key, 12)
    amplitude = jnp.exp(jax.random.uniform(scale_key, (EVENTS, 1), jnp.float32, math.log(0.3), math.log(3.0)))
    values = amplitude * jax.random.normal(shape_key, (EVENTS, W), jnp.float32)
    return jnp.clip(values, -16.0, 16.0).astype(jnp.bfloat16)


def draw_live_counts(key, part):
    count_key = jax.random.fold_in(key, 21)
    full_key = jax.random.fold_in(key, 22)
    counts = jax.random.randint(count_key, (BLOCKS,), EB // 2, EB + 1)
    full_block = jax.random.randint(full_key, (), 0, BLOCKS)
    positions = jnp.arange(BLOCKS, dtype=jnp.int32)
    return jnp.where(positions == full_block, EB, counts).astype(jnp.int32)


def place_ends(drawn, own_key, smallest, high):
    place = [jax.random.randint(jax.random.fold_in(own_key, axis), (), 0, length) for axis, length in enumerate(drawn.shape)]
    widest = drawn.shape.index(max(drawn.shape))
    neighbour = place[:widest] + [(place[widest] + 1) % drawn.shape[widest]] + place[widest + 1:]
    return drawn.at[tuple(place)].set(smallest).at[tuple(neighbour)].set(high)


def gaussian(stream_key, shape, deviation, bound, held_as=jnp.bfloat16):
    return jnp.clip(deviation * jax.random.normal(stream_key, shape, jnp.float32), -bound, bound).astype(held_as)


def setup_inputs(seed: int = 0) -> dict:
    key_of = jax.random.split(jax.random.key(seed), 5)
    return {
        "records": draw_records(jax.random.fold_in(key_of[4], 71), 0),
        "filter_taps": gaussian(key_of[1], (TAPS,), TAPS ** -0.5, 0.75),
        "live_counts": draw_live_counts(jax.random.fold_in(key_of[4], 71), 0),
        "pair_valid": place_ends((jax.random.randint(key_of[3], (BLOCKS, REACH), 0, 4) < 3).astype(jnp.int32), jax.random.fold_in(key_of[3], 1), 0, 1),
    }


epsilon = 1e-06

def band_matrix(filter_taps, samples):
    half_taps = (filter_taps.shape[0] - 1) // 2
    period = 2 * samples - 1
    spread = jnp.zeros((period,), jnp.float32)
    spread = lax.dynamic_update_slice(spread, filter_taps.astype(jnp.float32), (samples - 1 - half_taps,))
    repeated = jnp.tile(spread, samples + 1)[:samples * (period + 1)]
    hankel = repeated.reshape(samples, period + 1)[:, :samples]
    return hankel[:, ::-1].astype(jnp.bfloat16)

def correlate(own_block, own_scale, partner, weight):
    samples = own_block.shape[1]
    partner_scale = lax.rsqrt(lax.optimization_barrier(jnp.sum(jnp.square(partner.astype(jnp.float32)), axis=1)) + epsilon)
    padded = jnp.pad(partner, ((0, 0), (HALF, HALF)))
    products = [lax.dot_general(own_block, padded[:, lag_index:lag_index + samples], (((1,), (1,)), ((), ())), preferred_element_type=jnp.float32) for lag_index in range(2 * HALF + 1)]
    stacked = jnp.stack(products, axis=1)
    return (stacked * own_scale[:, None, None] * partner_scale[None, None, :] * weight).astype(jnp.bfloat16)

def reference(records, filter_taps, live_counts, pair_valid):
    blocked = records.reshape(BLOCKS, EB, W)
    live_rows = jnp.arange(EB, dtype=jnp.int32)[None, :] < live_counts[:, None]
    kept_rows = jnp.where(live_rows[:, :, None], blocked, jnp.zeros((), records.dtype))
    matrix = band_matrix(filter_taps, W)
    filtered = jnp.dot(kept_rows.reshape(EVENTS, W), matrix, preferred_element_type=jnp.float32).astype(jnp.bfloat16).reshape(BLOCKS, EB, W)
    scales = lax.rsqrt(lax.optimization_barrier(jnp.sum(jnp.square(filtered.astype(jnp.float32)), axis=2)) + epsilon)
    extended = jnp.concatenate([filtered, jnp.zeros((REACH, EB, W), filtered.dtype)], axis=0)

    def one_block(block_index):
        own_block = filtered[block_index]
        own_scale = scales[block_index]
        pieces = []
        for distance in range(REACH + 1):
            partner = lax.dynamic_index_in_dim(extended, block_index + distance, 0, keepdims=False)
            if distance == 0:
                weight = jnp.ones((), jnp.float32)
            else:
                weight = pair_valid[block_index, distance - 1].astype(jnp.float32)
            pieces.append(correlate(own_block, own_scale, partner, weight))
        return jnp.stack(pieces, axis=1)
    result = lax.map(one_block, jnp.arange(BLOCKS, dtype=jnp.int32))
    return result.reshape(EVENTS, REACH + 1, 2 * HALF + 1, EB)
```

```python
import functools

import jax
import jax.numpy as jnp
from jax import lax
from jax.experimental import pallas as pl
from jax.experimental.pallas import tpu as pltpu
from jax.sharding import PartitionSpec as P


HALF = 12
LAGS = 2 * HALF + 1
EPSILON = 1e-06
LANES = 128
CHUNK = 5
VMEM_MIB = 16


VMEM = pl.BlockSpec(memory_space=pltpu.VMEM)
SMEM = pl.BlockSpec(memory_space=pltpu.SMEM)
ANY = pl.BlockSpec(memory_space=pl.ANY)
HBM = pl.BlockSpec(memory_space=pltpu.HBM)


def in_hbm(array):
    return pltpu.with_memory_space_constraint(array, pltpu.HBM)


def params():
    return pltpu.CompilerParams(vmem_limit_bytes=VMEM_MIB << 20)


def filter_kernel(live_ref, taps_hbm, records_hbm, own_ref, taps_ref, records_ref, row_ref, band_ref, sems):
    events, samples = records_ref.shape
    copies = [
        pltpu.make_async_copy(source, target, sems.at[i])
        for i, (source, target) in enumerate(
            ((taps_hbm, taps_ref), (records_hbm, records_ref))
        )
    ]
    for copy in copies:
        copy.start()
    copies[0].wait()
    taps = taps_ref.shape[1]
    half_taps = (taps - 1) // 2
    row_ref[...] = jnp.zeros_like(row_ref)
    row_ref[0:1, 0:taps] = taps_ref[...].astype(jnp.float32)
    first = pltpu.roll(row_ref[0:1, :], LANES - half_taps, 1)
    spread = jnp.broadcast_to(first, (LANES, LANES))
    circulant = pltpu.roll(spread, 0, 1, stride=1, stride_axis=0)
    t = lax.broadcasted_iota(jnp.int32, (LANES, LANES), 0)
    u = lax.broadcasted_iota(jnp.int32, (LANES, LANES), 1)
    zero = jnp.zeros((), jnp.float32)
    ahead = u - t
    near = jnp.where(jnp.abs(ahead) <= half_taps, circulant, zero).astype(jnp.bfloat16)
    before = jnp.where(ahead >= LANES - half_taps, circulant, zero).astype(jnp.bfloat16)
    after = jnp.where(ahead <= half_taps - LANES, circulant, zero).astype(jnp.bfloat16)
    none = jnp.zeros((LANES, LANES), jnp.bfloat16)
    tiles = samples // LANES
    for i in range(tiles):
        for j in range(tiles):
            tile = {0: near, -1: before, 1: after}.get(j - i, none)
            band_ref[i * LANES : (i + 1) * LANES, j * LANES : (j + 1) * LANES] = tile
    copies[1].wait()
    row = lax.broadcasted_iota(jnp.int32, (events, samples), 0)
    records = records_ref[...]
    kept = jnp.where(row < live_ref[0], records, jnp.zeros((), records.dtype))
    own_ref[...] = lax.dot_general(
        kept, band_ref[...], (((1,), (1,)), ((), ())), preferred_element_type=jnp.float32
    ).astype(jnp.bfloat16)


def filtered(records, filter_taps, live_counts):
    events, samples = records.shape
    return pl.pallas_call(
        filter_kernel,
        out_shape=jax.ShapeDtypeStruct((events, samples), jnp.bfloat16),
        in_specs=[SMEM, HBM, HBM],
        out_specs=VMEM,
        scratch_shapes=[
            pltpu.VMEM((1, filter_taps.shape[0]), jnp.bfloat16),
            pltpu.VMEM((events, samples), jnp.bfloat16),
            pltpu.VMEM((8, LANES), jnp.float32),
            pltpu.VMEM((samples, samples), jnp.bfloat16),
            pltpu.SemaphoreType.DMA((2,)),
        ],
        compiler_params=params(),
        name="filter_rows",
    )(live_counts, in_hbm(filter_taps.reshape(1, -1)), in_hbm(records))


def shift_kernel(count, valid_hbm, own_ref, shifted_ref, scale_ref, weight_ref, valid_ref, sem):
    events, samples = own_ref.shape
    copy = pltpu.make_async_copy(valid_hbm, valid_ref, sem)
    copy.start()
    own = own_ref[...].astype(jnp.float32)
    total = jnp.sum(own * own, axis=1, keepdims=True)
    scale_ref[...] = jnp.broadcast_to(lax.rsqrt(total + EPSILON), scale_ref.shape)
    padded = jnp.concatenate([own, jnp.zeros((events, LANES), jnp.float32)], axis=1)
    width = samples + LANES
    for lag in range(LAGS):
        moved = pltpu.roll(padded, (lag - HALF) % width, 1)[:, :samples]
        shifted_ref[lag * events : (lag + 1) * events, :] = moved.astype(jnp.bfloat16)
    copy.wait()
    me = lax.axis_index("ev")
    weight_ref[0:1, :] = jnp.ones((1, LANES), jnp.float32)
    for k in range(1, valid_hbm.shape[1] + 1):
        weight = jnp.where(me + k < count, valid_ref[0, k - 1].astype(jnp.float32), 0.0)
        weight_ref[k : k + 1, :] = jnp.full((1, LANES), weight, jnp.float32)


def shifted_rows(own, pair_valid, count):
    events, samples = own.shape
    slabs = pair_valid.shape[1] + 1
    return pl.pallas_call(
        functools.partial(shift_kernel, count),
        out_shape=(
            jax.ShapeDtypeStruct((LAGS * events, samples), jnp.bfloat16),
            jax.ShapeDtypeStruct((events, LANES), jnp.float32),
            jax.ShapeDtypeStruct((slabs, LANES), jnp.float32),
        ),
        in_specs=[HBM, VMEM],
        out_specs=(VMEM, VMEM, VMEM),
        scratch_shapes=[pltpu.SMEM(pair_valid.shape, jnp.int32), pltpu.SemaphoreType.DMA],
        compiler_params=params(),
        cost_estimate=pl.CostEstimate(flops=0, transcendentals=0, bytes_accessed=3 << 20),
        name="shift_rows",
    )(in_hbm(pair_valid), own)


def row_scale(block):
    square = jnp.square(block.astype(jnp.float32))
    high = square.astype(jnp.bfloat16)
    low = (square - high.astype(jnp.float32)).astype(jnp.bfloat16)
    ones = jnp.ones((8, block.shape[1]), jnp.bfloat16)
    over = (((1,), (1,)), ((), ()))
    total = lax.dot_general(ones, high, over, preferred_element_type=jnp.float32)
    total += lax.dot_general(ones, low, over, preferred_element_type=jnp.float32)
    return lax.rsqrt(total[0:1] + EPSILON)


def slots_of(slabs):
    core = lax.rem(lax.axis_index("ev"), 2)
    return [k if isinstance(k, int) else jnp.where(core == 0, k[0], k[1]) for k in slabs]


def pair_kernel(slabs, places, before, parts, last, shifted_ref, scale_ref, weight_ref, one_ref, two_ref, *rest):
    rest = list(rest)
    before_ref = None
    if before is not None:
        before_ref = rest.pop(0)
        rest.pop(0)
    out_ref, block_ref, factor_ref, before_sems, sems = rest
    events = scale_ref.shape[0]
    copies = []
    if before is not None:
        for i, k in enumerate(slots_of(before)):
            copy = pltpu.make_async_copy(before_ref.at[i], out_ref.at[k], before_sems.at[i])
            copy.start()
            copies.append(copy)
    always = lax.axis_index("ev") >= 0
    slots = slots_of(slabs)
    blocks = [ref if place is None else ref.at[place] for ref, place in zip((one_ref, two_ref), places)]

    def compute(start, stop, begin):
        partners = jnp.concatenate([block[...] for block in blocks], axis=0)
        if begin:
            scales = row_scale(partners)
            for i, k in enumerate(slots):
                part = scales[:, i * events : (i + 1) * events] * weight_ref[pl.ds(k, 1), :]
                factor_ref[i] = scale_ref[...] * part
        for low in range(start, stop, CHUNK):
            lags = slice(low, low + CHUNK)
            product = lax.dot_general(
                shifted_ref[low * events : (low + CHUNK) * events, :],
                partners,
                (((1,), (1,)), ((), ())),
                preferred_element_type=jnp.float32,
            )
            for i in range(2):
                piece = product[:, i * events : (i + 1) * events].reshape(CHUNK, events, events)
                block_ref[i, lags] = (piece * factor_ref[i][None]).astype(jnp.bfloat16)

    for n, (start, stop) in enumerate(parts):
        pl.when(always)(functools.partial(compute, start, stop, n == 0))
        if last:
            for i, k in enumerate(slots):
                copy = pltpu.make_async_copy(
                    block_ref.at[i, start:stop], out_ref.at[k, start:stop], sems.at[i, n]
                )
                copy.start()
                copies.append(copy)
    for copy in copies:
        copy.wait()


def correlate_pair(carried, slabs, blocks, places, held, last=False):
    shifted, scale, weight = held
    events = scale.shape[0]
    operands = [shifted, scale, weight, *blocks]
    in_specs = [VMEM] * 5
    aliases = {}
    before = None
    if carried is not None:
        out, before, block = carried
        operands += [block, out]
        in_specs += [VMEM, ANY]
        aliases = {6: 0}
    parts = ((0, 10), (10, 20), (20, LAGS)) if last else ((0, LAGS),)
    block = (2, LAGS, events, events)
    out_shape = [jax.ShapeDtypeStruct((weight.shape[0], LAGS, events, events), jnp.bfloat16)]
    out_specs = [ANY]
    scratch = [
        pltpu.VMEM((2, events, events), jnp.float32),
        pltpu.SemaphoreType.DMA((2,)),
        pltpu.SemaphoreType.DMA((2, len(parts))),
    ]
    if last:
        scratch.insert(0, pltpu.VMEM(block, jnp.bfloat16))
    else:
        out_shape.append(jax.ShapeDtypeStruct(block, jnp.bfloat16))
        out_specs.append(VMEM)
    result = pl.pallas_call(
        functools.partial(pair_kernel, slabs, places, before, parts, last),
        out_shape=out_shape,
        in_specs=in_specs,
        out_specs=out_specs,
        scratch_shapes=scratch,
        input_output_aliases=aliases,
        compiler_params=params(),
        cost_estimate=pl.CostEstimate(
            flops=4 * LAGS * events * events * shifted.shape[1],
            transcendentals=0,
            bytes_accessed=4 * LAGS * events * events,
        ),
        name="pair",
    )(*operands)
    return (result[0], slabs, None if last else result[1])


def permuted(block, target):
    count = lax.axis_size("ev")
    return lax.ppermute(block, "ev", [(s, target(s) % count) for s in range(count)])


def along_row(step):
    def target(s):
        return s // 8 * 8 + (s % 8 - 2 * step) % 8

    return target


def whole(records, filter_taps, live_counts, pair_valid):
    count = lax.axis_size("ev")
    own = filtered(records, filter_taps, live_counts)
    chip = lax.rem(lax.axis_index("ev") // 2, 4)

    above = permuted(own, lambda s: s - 8)
    mixed = permuted(own, lambda s: s - 1 if s % 2 else s - 9)
    held = shifted_rows(own, pair_valid, count)

    def swapped(block):
        return permuted(block, lambda s: s ^ 1)

    def ahead(step):
        payload = jnp.where(chip >= step, own, above)
        return permuted(payload, along_row(step))

    x1 = ahead(1)
    x3 = ahead(3)
    x2 = ahead(2)
    three_s = swapped(jnp.stack([above, x1, x3]))
    x2_s = swapped(x2)
    none = (None, None)
    carried = correlate_pair(None, (0, 8), (own, above), none, held)
    carried = correlate_pair(carried, (2, 6), (x1, x3), none, held)
    carried = correlate_pair(carried, ((1, 9), (9, 7)), (mixed, three_s), (None, 0), held)
    carried = correlate_pair(carried, ((3, 1), (7, 5)), (three_s, three_s), (1, 2), held)
    carried = correlate_pair(carried, (4, (5, 3)), (x2, x2_s), none, held, last=True)
    return carried[0].transpose(2, 0, 1, 3)


def solution(mesh):
    in_specs = (P("ev", None), P(), P("ev"), P("ev", None))
    out_specs = P("ev", None, None, None)
    return jax.shard_map(whole, mesh=mesh, in_specs=in_specs, out_specs=out_specs, check_vma=False)
```

```python
import functools

import jax
import jax.numpy as jnp
from jax import lax
from jax.experimental import pallas as pl
from jax.experimental.pallas import tpu as pltpu
from jax.sharding import PartitionSpec as P


HALF = 12
LAGS = 2 * HALF + 1
EPSILON = 1e-06
LANES = 128
CHUNK = 5
VMEM_MIB = 16


VMEM = pl.BlockSpec(memory_space=pltpu.VMEM)
SMEM = pl.BlockSpec(memory_space=pltpu.SMEM)
ANY = pl.BlockSpec(memory_space=pl.ANY)
HBM = pl.BlockSpec(memory_space=pltpu.HBM)


def in_hbm(array):
    return pltpu.with_memory_space_constraint(array, pltpu.HBM)


def params():
    return pltpu.CompilerParams(vmem_limit_bytes=VMEM_MIB << 20)


def filter_kernel(live_ref, taps_hbm, records_hbm, own_ref, taps_ref, records_ref, row_ref, band_ref, sems):
    events, samples = records_ref.shape
    copies = [
        pltpu.make_async_copy(source, target, sems.at[i])
        for i, (source, target) in enumerate(
            ((taps_hbm, taps_ref), (records_hbm, records_ref))
        )
    ]
    for copy in copies:
        copy.start()
    copies[0].wait()
    taps = taps_ref.shape[1]
    half_taps = (taps - 1) // 2
    row_ref[...] = jnp.zeros_like(row_ref)
    row_ref[0:1, 0:taps] = taps_ref[...].astype(jnp.float32)
    first = pltpu.roll(row_ref[0:1, :], LANES - half_taps, 1)
    spread = jnp.broadcast_to(first, (LANES, LANES))
    circulant = pltpu.roll(spread, 0, 1, stride=1, stride_axis=0)
    t = lax.broadcasted_iota(jnp.int32, (LANES, LANES), 0)
    u = lax.broadcasted_iota(jnp.int32, (LANES, LANES), 1)
    zero = jnp.zeros((), jnp.float32)
    ahead = u - t
    near = jnp.where(jnp.abs(ahead) <= half_taps, circulant, zero).astype(jnp.bfloat16)
    before = jnp.where(ahead >= LANES - half_taps, circulant, zero).astype(jnp.bfloat16)
    after = jnp.where(ahead <= half_taps - LANES, circulant, zero).astype(jnp.bfloat16)
    none = jnp.zeros((LANES, LANES), jnp.bfloat16)
    tiles = samples // LANES
    for i in range(tiles):
        for j in range(tiles):
            tile = {0: near, -1: before, 1: after}.get(j - i, none)
            band_ref[i * LANES : (i + 1) * LANES, j * LANES : (j + 1) * LANES] = tile
    copies[1].wait()
    row = lax.broadcasted_iota(jnp.int32, (events, samples), 0)
    records = records_ref[...]
    kept = jnp.where(row < live_ref[0], records, jnp.zeros((), records.dtype))
    own_ref[...] = lax.dot_general(
        kept, band_ref[...], (((1,), (1,)), ((), ())), preferred_element_type=jnp.float32
    ).astype(jnp.bfloat16)


def filtered(records, filter_taps, live_counts):
    events, samples = records.shape
    return pl.pallas_call(
        filter_kernel,
        out_shape=jax.ShapeDtypeStruct((events, samples), jnp.bfloat16),
        in_specs=[SMEM, HBM, HBM],
        out_specs=VMEM,
        scratch_shapes=[
            pltpu.VMEM((1, filter_taps.shape[0]), jnp.bfloat16),
            pltpu.VMEM((events, samples), jnp.bfloat16),
            pltpu.VMEM((8, LANES), jnp.float32),
            pltpu.VMEM((samples, samples), jnp.bfloat16),
            pltpu.SemaphoreType.DMA((2,)),
        ],
        compiler_params=params(),
        name="filter_rows",
    )(live_counts, in_hbm(filter_taps.reshape(1, -1)), in_hbm(records))


def shift_kernel(count, valid_hbm, own_ref, shifted_ref, scale_ref, weight_ref, valid_ref, sem):
    events, samples = own_ref.shape
    copy = pltpu.make_async_copy(valid_hbm, valid_ref, sem)
    copy.start()
    own = own_ref[...].astype(jnp.float32)
    total = jnp.sum(own * own, axis=1, keepdims=True)
    scale_ref[...] = jnp.broadcast_to(lax.rsqrt(total + EPSILON), scale_ref.shape)
    padded = jnp.concatenate([own, jnp.zeros((events, LANES), jnp.float32)], axis=1)
    width = samples + LANES
    for lag in range(LAGS):
        moved = pltpu.roll(padded, (lag - HALF) % width, 1)[:, :samples]
        shifted_ref[lag * events : (lag + 1) * events, :] = moved.astype(jnp.bfloat16)
    copy.wait()
    me = lax.axis_index("ev")
    weight_ref[0:1, :] = jnp.ones((1, LANES), jnp.float32)
    for k in range(1, valid_hbm.shape[1] + 1):
        weight = jnp.where(me + k < count, valid_ref[0, k - 1].astype(jnp.float32), 0.0)
        weight_ref[k : k + 1, :] = jnp.full((1, LANES), weight, jnp.float32)


def shifted_rows(own, pair_valid, count):
    events, samples = own.shape
    slabs = pair_valid.shape[1] + 1
    return pl.pallas_call(
        functools.partial(shift_kernel, count),
        out_shape=(
            jax.ShapeDtypeStruct((LAGS * events, samples), jnp.bfloat16),
            jax.ShapeDtypeStruct((events, LANES), jnp.float32),
            jax.ShapeDtypeStruct((slabs, LANES), jnp.float32),
        ),
        in_specs=[HBM, VMEM],
        out_specs=(VMEM, VMEM, VMEM),
        scratch_shapes=[pltpu.SMEM(pair_valid.shape, jnp.int32), pltpu.SemaphoreType.DMA],
        compiler_params=params(),
        cost_estimate=pl.CostEstimate(flops=0, transcendentals=0, bytes_accessed=3 << 20),
        name="shift_rows",
    )(in_hbm(pair_valid), own)


def row_scale(block):
    square = jnp.square(block.astype(jnp.float32))
    high = square.astype(jnp.bfloat16)
    low = (square - high.astype(jnp.float32)).astype(jnp.bfloat16)
    ones = jnp.ones((8, block.shape[1]), jnp.bfloat16)
    over = (((1,), (1,)), ((), ()))
    total = lax.dot_general(ones, high, over, preferred_element_type=jnp.float32)
    total += lax.dot_general(ones, low, over, preferred_element_type=jnp.float32)
    return lax.rsqrt(total[0:1] + EPSILON)


def slots_of(slabs):
    place = lax.rem(lax.axis_index("ev"), 4)

    def slot(k):
        if isinstance(k, int):
            return k
        if len(k) == 2:
            return jnp.where(lax.rem(place, 2) == 0, k[0], k[1])
        return jnp.where(place == 0, k[0], jnp.where(place == 1, k[1], jnp.where(place == 2, k[2], k[3])))

    return [slot(k) for k in slabs]


def pair_kernel(slabs, places, before, parts, sent, shifted_ref, scale_ref, weight_ref, one_ref, two_ref, *rest):
    rest = list(rest)
    before_ref = None
    if before is not None:
        before_ref = rest.pop(0)
        rest.pop(0)
    out_ref, block_ref, factor_ref, before_sems, sems = rest
    events = scale_ref.shape[0]
    copies = []
    if before is not None:
        left = slice(before[1], LAGS)
        for i, k in enumerate(slots_of(before[0])):
            copy = pltpu.make_async_copy(before_ref.at[i, left], out_ref.at[k, left], before_sems.at[i])
            copy.start()
            copies.append(copy)
    always = lax.axis_index("ev") >= 0
    slots = slots_of(slabs)
    blocks = [ref if place is None else ref.at[place] for ref, place in zip((one_ref, two_ref), places)]

    def compute(start, stop, begin):
        partners = jnp.concatenate([block[...] for block in blocks], axis=0)
        if begin:
            scales = row_scale(partners)
            for i, k in enumerate(slots):
                part = scales[:, i * events : (i + 1) * events] * weight_ref[pl.ds(k, 1), :]
                factor_ref[i] = scale_ref[...] * part
        for low in range(start, stop, CHUNK):
            lags = slice(low, low + CHUNK)
            product = lax.dot_general(
                shifted_ref[low * events : (low + CHUNK) * events, :],
                partners,
                (((1,), (1,)), ((), ())),
                preferred_element_type=jnp.float32,
            )
            for i in range(2):
                piece = product[:, i * events : (i + 1) * events].reshape(CHUNK, events, events)
                block_ref[i, lags] = (piece * factor_ref[i][None]).astype(jnp.bfloat16)

    for n, (start, stop) in enumerate(parts):
        pl.when(always)(functools.partial(compute, start, stop, n == 0))
        if n < sent:
            for i, k in enumerate(slots):
                copy = pltpu.make_async_copy(
                    block_ref.at[i, start:stop], out_ref.at[k, start:stop], sems.at[i, n]
                )
                copy.start()
                copies.append(copy)
    for copy in copies:
        copy.wait()


def correlate_pair(carried, slabs, blocks, places, held, parts=((0, LAGS),), sent=0):
    shifted, scale, weight = held
    events = scale.shape[0]
    operands = [shifted, scale, weight, *blocks]
    in_specs = [VMEM] * 5
    aliases = {}
    before = None
    if carried is not None:
        out, before, block = carried
        operands += [block, out]
        in_specs += [VMEM, ANY]
        aliases = {6: 0}
    last = sent == len(parts)
    block = (2, LAGS, events, events)
    out_shape = [jax.ShapeDtypeStruct((weight.shape[0], LAGS, events, events), jnp.bfloat16)]
    out_specs = [ANY]
    scratch = [
        pltpu.VMEM((2, events, events), jnp.float32),
        pltpu.SemaphoreType.DMA((2,)),
        pltpu.SemaphoreType.DMA((2, len(parts))),
    ]
    if last:
        scratch.insert(0, pltpu.VMEM(block, jnp.bfloat16))
    else:
        out_shape.append(jax.ShapeDtypeStruct(block, jnp.bfloat16))
        out_specs.append(VMEM)
    result = pl.pallas_call(
        functools.partial(pair_kernel, slabs, places, before, parts, sent),
        out_shape=out_shape,
        in_specs=in_specs,
        out_specs=out_specs,
        scratch_shapes=scratch,
        input_output_aliases=aliases,
        compiler_params=params(),
        cost_estimate=pl.CostEstimate(
            flops=4 * LAGS * events * events * shifted.shape[1],
            transcendentals=0,
            bytes_accessed=4 * LAGS * events * events,
        ),
        name="pair",
    )(*operands)
    return (result[0], (slabs, parts[sent - 1][1] if sent else 0), None if last else result[1])


def permuted(block, target):
    count = lax.axis_size("ev")
    return lax.ppermute(block, "ev", [(s, target(s) % count) for s in range(count)])


def along_row(step):
    return lambda s: s ^ (2 * step)


def whole(records, filter_taps, live_counts, pair_valid):
    count = lax.axis_size("ev")
    own = filtered(records, filter_taps, live_counts)
    chip = lax.rem(lax.axis_index("ev") // 2, 4)

    above = permuted(own, lambda s: s - 8)
    mixed = permuted(own, lambda s: s - 1 if s % 2 else s - 9)
    held = shifted_rows(own, pair_valid, count)

    def swapped(block):
        return permuted(block, lambda s: s ^ 1)

    def ahead(step):
        payload = jnp.where(chip > jnp.bitwise_xor(chip, step), own, above)
        return permuted(payload, along_row(step))

    x1 = ahead(1)
    x3 = ahead(3)
    x2 = ahead(2)
    above_s = swapped(above)
    x1_s = swapped(x1)
    two_s = swapped(jnp.stack([x3, x2]))
    none = (None, None)
    carried = correlate_pair(None, (0, 8), (own, above), none, held)
    carried = correlate_pair(carried, ((1, 9), (9, 7)), (mixed, above_s), none, held)
    carried = correlate_pair(carried, ((2, 2, 6, 6), (3, 1, 7, 5)), (x1, x1_s), none, held)
    carried = correlate_pair(carried, ((6, 6, 2, 2), 4), (x3, x2), none, held)
    parts = ((0, 15), (15, LAGS))
    carried = correlate_pair(carried, ((7, 5, 3, 1), (5, 3)), (two_s, two_s), (0, 1), held, parts, 2)
    return carried[0].transpose(2, 0, 1, 3)


def solution(mesh):
    in_specs = (P("ev", None), P(), P("ev"), P("ev", None))
    out_specs = P("ev", None, None, None)
    return jax.shard_map(whole, mesh=mesh, in_specs=in_specs, out_specs=out_specs, check_vma=False)
```

```python
import functools

import jax
import jax.numpy as jnp
from jax import lax
from jax.experimental import pallas as pl
from jax.experimental.pallas import tpu as pltpu
from jax.sharding import PartitionSpec as P


HALF = 12
LAGS = 2 * HALF + 1
EPSILON = 1e-06
LANES = 128
CHUNK = 5
VMEM_MIB = 16


VMEM = pl.BlockSpec(memory_space=pltpu.VMEM)
SMEM = pl.BlockSpec(memory_space=pltpu.SMEM)
ANY = pl.BlockSpec(memory_space=pl.ANY)
HBM = pl.BlockSpec(memory_space=pltpu.HBM)


def in_hbm(array):
    return pltpu.with_memory_space_constraint(array, pltpu.HBM)


def params():
    return pltpu.CompilerParams(vmem_limit_bytes=VMEM_MIB << 20)


def filter_kernel(live_ref, taps_hbm, records_hbm, own_ref, taps_ref, records_ref, row_ref, band_ref, sems):
    events, samples = records_ref.shape
    copies = [
        pltpu.make_async_copy(source, target, sems.at[i])
        for i, (source, target) in enumerate(
            ((taps_hbm, taps_ref), (records_hbm, records_ref))
        )
    ]
    for copy in copies:
        copy.start()
    copies[0].wait()
    taps = taps_ref.shape[1]
    half_taps = (taps - 1) // 2
    row_ref[...] = jnp.zeros_like(row_ref)
    row_ref[0:1, 0:taps] = taps_ref[...].astype(jnp.float32)
    first = pltpu.roll(row_ref[0:1, :], LANES - half_taps, 1)
    spread = jnp.broadcast_to(first, (LANES, LANES))
    circulant = pltpu.roll(spread, 0, 1, stride=1, stride_axis=0)
    t = lax.broadcasted_iota(jnp.int32, (LANES, LANES), 0)
    u = lax.broadcasted_iota(jnp.int32, (LANES, LANES), 1)
    zero = jnp.zeros((), jnp.float32)
    ahead = u - t
    near = jnp.where(jnp.abs(ahead) <= half_taps, circulant, zero).astype(jnp.bfloat16)
    before = jnp.where(ahead >= LANES - half_taps, circulant, zero).astype(jnp.bfloat16)
    after = jnp.where(ahead <= half_taps - LANES, circulant, zero).astype(jnp.bfloat16)
    none = jnp.zeros((LANES, LANES), jnp.bfloat16)
    tiles = samples // LANES
    for i in range(tiles):
        for j in range(tiles):
            tile = {0: near, -1: before, 1: after}.get(j - i, none)
            band_ref[i * LANES : (i + 1) * LANES, j * LANES : (j + 1) * LANES] = tile
    copies[1].wait()
    row = lax.broadcasted_iota(jnp.int32, (events, samples), 0)
    records = records_ref[...]
    kept = jnp.where(row < live_ref[0], records, jnp.zeros((), records.dtype))
    own_ref[...] = lax.dot_general(
        kept, band_ref[...], (((1,), (1,)), ((), ())), preferred_element_type=jnp.float32
    ).astype(jnp.bfloat16)


def filtered(records, filter_taps, live_counts):
    events, samples = records.shape
    return pl.pallas_call(
        filter_kernel,
        out_shape=jax.ShapeDtypeStruct((events, samples), jnp.bfloat16),
        in_specs=[SMEM, HBM, HBM],
        out_specs=VMEM,
        scratch_shapes=[
            pltpu.VMEM((1, filter_taps.shape[0]), jnp.bfloat16),
            pltpu.VMEM((events, samples), jnp.bfloat16),
            pltpu.VMEM((8, LANES), jnp.float32),
            pltpu.VMEM((samples, samples), jnp.bfloat16),
            pltpu.SemaphoreType.DMA((2,)),
        ],
        compiler_params=params(),
        name="filter_rows",
    )(live_counts, in_hbm(filter_taps.reshape(1, -1)), in_hbm(records))


def shift_kernel(count, valid_hbm, own_ref, shifted_ref, scale_ref, weight_ref, valid_ref, sem):
    events, samples = own_ref.shape
    copy = pltpu.make_async_copy(valid_hbm, valid_ref, sem)
    copy.start()
    own = own_ref[...].astype(jnp.float32)
    total = jnp.sum(own * own, axis=1, keepdims=True)
    scale_ref[...] = jnp.broadcast_to(lax.rsqrt(total + EPSILON), scale_ref.shape)
    padded = jnp.concatenate([own, jnp.zeros((events, LANES), jnp.float32)], axis=1)
    width = samples + LANES
    for lag in range(LAGS):
        moved = pltpu.roll(padded, (lag - HALF) % width, 1)[:, :samples]
        shifted_ref[lag * events : (lag + 1) * events, :] = moved.astype(jnp.bfloat16)
    copy.wait()
    me = lax.axis_index("ev")
    weight_ref[0:1, :] = jnp.ones((1, LANES), jnp.float32)
    for k in range(1, valid_hbm.shape[1] + 1):
        weight = jnp.where(me + k < count, valid_ref[0, k - 1].astype(jnp.float32), 0.0)
        weight_ref[k : k + 1, :] = jnp.full((1, LANES), weight, jnp.float32)


def shifted_rows(own, pair_valid, count):
    events, samples = own.shape
    slabs = pair_valid.shape[1] + 1
    return pl.pallas_call(
        functools.partial(shift_kernel, count),
        out_shape=(
            jax.ShapeDtypeStruct((LAGS * events, samples), jnp.bfloat16),
            jax.ShapeDtypeStruct((events, LANES), jnp.float32),
            jax.ShapeDtypeStruct((slabs, LANES), jnp.float32),
        ),
        in_specs=[HBM, VMEM],
        out_specs=(VMEM, VMEM, VMEM),
        scratch_shapes=[pltpu.SMEM(pair_valid.shape, jnp.int32), pltpu.SemaphoreType.DMA],
        compiler_params=params(),
        cost_estimate=pl.CostEstimate(flops=0, transcendentals=0, bytes_accessed=3 << 20),
        name="shift_rows",
    )(in_hbm(pair_valid), own)


def row_scale(block):
    square = jnp.square(block.astype(jnp.float32))
    high = square.astype(jnp.bfloat16)
    low = (square - high.astype(jnp.float32)).astype(jnp.bfloat16)
    ones = jnp.ones((8, block.shape[1]), jnp.bfloat16)
    over = (((1,), (1,)), ((), ()))
    total = lax.dot_general(ones, high, over, preferred_element_type=jnp.float32)
    total += lax.dot_general(ones, low, over, preferred_element_type=jnp.float32)
    return lax.rsqrt(total[0:1] + EPSILON)


def slots_of(slabs):
    place = lax.rem(lax.axis_index("ev"), 4)

    def slot(k):
        if isinstance(k, int):
            return k
        if len(k) == 2:
            return jnp.where(lax.rem(place, 2) == 0, k[0], k[1])
        return jnp.where(place == 0, k[0], jnp.where(place == 1, k[1], jnp.where(place == 2, k[2], k[3])))

    return [slot(k) for k in slabs]


def pair_kernel(slabs, places, before, parts, sent, shifted_ref, scale_ref, weight_ref, one_ref, two_ref, *rest):
    rest = list(rest)
    before_ref = None
    if before is not None:
        before_ref = rest.pop(0)
        rest.pop(0)
    out_ref, block_ref, factor_ref, before_sems, sems = rest
    events = scale_ref.shape[0]
    copies = []
    if before is not None:
        left = slice(before[1], LAGS)
        for i, k in enumerate(slots_of(before[0])):
            copy = pltpu.make_async_copy(before_ref.at[i, left], out_ref.at[k, left], before_sems.at[i])
            copy.start()
            copies.append(copy)
    always = lax.axis_index("ev") >= 0
    slots = slots_of(slabs)
    blocks = [ref if place is None else ref.at[place] for ref, place in zip((one_ref, two_ref), places)]

    def compute(start, stop, begin):
        partners = jnp.concatenate([block[...] for block in blocks], axis=0)
        if begin:
            scales = row_scale(partners)
            for i, k in enumerate(slots):
                part = scales[:, i * events : (i + 1) * events] * weight_ref[pl.ds(k, 1), :]
                factor_ref[i] = scale_ref[...] * part
        for low in range(start, stop, CHUNK):
            lags = slice(low, low + CHUNK)
            product = lax.dot_general(
                shifted_ref[low * events : (low + CHUNK) * events, :],
                partners,
                (((1,), (1,)), ((), ())),
                preferred_element_type=jnp.float32,
            )
            for i in range(2):
                piece = product[:, i * events : (i + 1) * events].reshape(CHUNK, events, events)
                block_ref[i, lags] = (piece * factor_ref[i][None]).astype(jnp.bfloat16)

    for n, (start, stop) in enumerate(parts):
        pl.when(always)(functools.partial(compute, start, stop, n == 0))
        if n < sent:
            for i, k in enumerate(slots):
                copy = pltpu.make_async_copy(
                    block_ref.at[i, start:stop], out_ref.at[k, start:stop], sems.at[i, n]
                )
                copy.start()
                copies.append(copy)
    for copy in copies:
        copy.wait()


def correlate_pair(carried, slabs, blocks, places, held, parts=((0, LAGS),), sent=0):
    shifted, scale, weight = held
    events = scale.shape[0]
    operands = [shifted, scale, weight, *blocks]
    in_specs = [VMEM] * 5
    aliases = {}
    before = None
    if carried is not None:
        out, before, block = carried
        operands += [block, out]
        in_specs += [VMEM, ANY]
        aliases = {6: 0}
    last = sent == len(parts)
    block = (2, LAGS, events, events)
    out_shape = [jax.ShapeDtypeStruct((weight.shape[0], LAGS, events, events), jnp.bfloat16)]
    out_specs = [ANY]
    scratch = [
        pltpu.VMEM((2, events, events), jnp.float32),
        pltpu.SemaphoreType.DMA((2,)),
        pltpu.SemaphoreType.DMA((2, len(parts))),
    ]
    if last:
        scratch.insert(0, pltpu.VMEM(block, jnp.bfloat16))
    else:
        out_shape.append(jax.ShapeDtypeStruct(block, jnp.bfloat16))
        out_specs.append(VMEM)
    result = pl.pallas_call(
        functools.partial(pair_kernel, slabs, places, before, parts, sent),
        out_shape=out_shape,
        in_specs=in_specs,
        out_specs=out_specs,
        scratch_shapes=scratch,
        input_output_aliases=aliases,
        compiler_params=params(),
        cost_estimate=pl.CostEstimate(
            flops=4 * LAGS * events * events * shifted.shape[1],
            transcendentals=0,
            bytes_accessed=4 * LAGS * events * events,
        ),
        name="pair",
    )(*operands)
    return (result[0], (slabs, parts[sent - 1][1] if sent else 0), None if last else result[1])


def permuted(block, target):
    count = lax.axis_size("ev")
    return lax.ppermute(block, "ev", [(s, target(s) % count) for s in range(count)])


def along_row(step):
    return lambda s: s ^ (2 * step)


def whole(records, filter_taps, live_counts, pair_valid):
    count = lax.axis_size("ev")
    own = filtered(records, filter_taps, live_counts)
    chip = lax.rem(lax.axis_index("ev") // 2, 4)

    above = permuted(own, lambda s: s - 8)
    mixed = permuted(own, lambda s: s - 1 if s % 2 else s - 9)
    held = shifted_rows(own, pair_valid, count)

    def swapped(block):
        return permuted(block, lambda s: s ^ 1)

    def ahead(step):
        payload = jnp.where(chip > jnp.bitwise_xor(chip, step), own, above)
        return permuted(payload, along_row(step))

    x1 = ahead(1)
    x3 = ahead(3)
    x2 = ahead(2)
    early_s = swapped(jnp.stack([above, x1]))
    two_s = swapped(jnp.stack([x3, x2]))
    none = (None, None)
    carried = correlate_pair(None, (0, 8), (own, above), none, held)
    carried = correlate_pair(carried, ((2, 2, 6, 6), (1, 9)), (x1, mixed), none, held)
    carried = correlate_pair(carried, ((9, 7), (3, 1, 7, 5)), (early_s, early_s), (0, 1), held)
    carried = correlate_pair(carried, ((6, 6, 2, 2), 4), (x3, x2), none, held)
    parts = ((0, 15), (15, LAGS))
    carried = correlate_pair(carried, ((7, 5, 3, 1), (5, 3)), (two_s, two_s), (0, 1), held, parts, 2)
    return carried[0].transpose(2, 0, 1, 3)


def solution(mesh):
    in_specs = (P("ev", None), P(), P("ev"), P("ev", None))
    out_specs = P("ev", None, None, None)
    return jax.shard_map(whole, mesh=mesh, in_specs=in_specs, out_specs=out_specs, check_vma=False)
```
